32 devices in a mesh: rows: 8 (over z, y), cols: 4 (over x, core).
Axes of the slice: x: 2, y: 2, z: 4, core: 2. Of those that a mesh axis runs over, the one named last changes fastest.
Arguments:
- vectors: float32 [16384, 512], P('rows', 'cols'), may hold values from -6 to 6
- reflectors: float32 [3, 128, 256, 128], P(None, ('rows', 'cols')), may hold values from -1.05 to 1.05, as said below
- factors: float32 [3, 128, 128, 128], P(None, ('rows', 'cols')), may hold values from -0.25 to 1.1, as said below
- starts: int32 [3, 128], P(None, 'rows'), may hold values from 0 to 16256, as said below
Outputs:
- transformed: float32 [16384, 512], P('rows', 'cols')
The draws below stay inside these ranges and needn't reach their ends.
Inputs may be any that keep to these rules, and one draw needn't show every extreme that they name: `reflectors`: each diamond's matrix is unit lower trapezoidal: entry (i, j) is 1 for i = j and 0 for i < j. `factors`: upper triangular; F is the compact-WY factor of the diamond's reflectors, the inverse of the upper triangle of V^T V with its diagonal halved, so that I - V F V^T is orthogonal. starts[t, g] lies between 128 * g and 128 * g + 64; for the first diamond and for the last diamond of every aligned block of 16 diamonds it equals 128 * g.
All inputs are finite; a program needn't handle non-finite values.
Results may differ from the reference program's by a relative error of at most 0.0003.
Values sent between devices are 32-bit elements; how exact they have to be, the bound alone decides.
A program may use at most 64 MiB of HBM per device.

```python
import jax
import jax.numpy as jnp
from jax import lax

BLOCK = 128
DIA_DEV = 16
TICKS = 3
NR = 16384
NC = 512
NDIA = 128


def householder_panel(key):
    key_lead, key_sign, key_noise = jax.random.split(jax.random.fold_in(key, 37), 3)
    shape = (TICKS, NDIA, 2 * BLOCK, BLOCK)
    spread = 0.05 / BLOCK ** 0.5
    noise = jnp.clip(jax.random.normal(key_noise, shape, jnp.float32), -4.0, 4.0) * spread
    magnitude = jax.random.uniform(key_lead, (TICKS, NDIA, BLOCK), jnp.float32, 0.97, 1.03)
    sign_bits = jax.random.randint(key_sign, (TICKS, NDIA, BLOCK), 0, 2, jnp.int32)
    partner = magnitude * (2 * sign_bits - 1).astype(jnp.float32)
    row_ids = jnp.arange(2 * BLOCK, dtype=jnp.int32)[:, None]
    col_ids = jnp.arange(BLOCK, dtype=jnp.int32)[None, :]
    is_diag = row_ids == col_ids
    is_partner = row_ids == col_ids + BLOCK
    is_below = row_ids > col_ids
    panel = jnp.where(is_below, noise, 0.0)
    panel = jnp.where(is_partner, partner[..., None, :], panel)
    panel = jnp.where(is_diag, 1.0, panel)
    return panel.astype(jnp.float32)


def draw_reflectors(key, part):
    return householder_panel(key)


def draw_factors(key, part):
    panel = householder_panel(key)
    gram = jnp.einsum('tgri,tgrj->tgij', panel, panel, precision=lax.Precision.HIGHEST)
    unit = jnp.eye(BLOCK, dtype=jnp.float32)
    inverse_factor = jnp.triu(gram, 1) + 0.5 * gram * unit
    identity_stack = jnp.broadcast_to(unit, inverse_factor.shape)
    factor = jnp.linalg.solve(inverse_factor, identity_stack)
    return jnp.triu(factor).astype(jnp.float32)


def draw_starts(key, part):
    shift_rows = jax.random.randint(jax.random.fold_in(key, 23), (TICKS, NDIA), 0, BLOCK // 2 + 1, jnp.int32)
    index_rows = jnp.arange(NDIA, dtype=jnp.int32)
    is_fixed = jnp.logical_or(index_rows % DIA_DEV == DIA_DEV - 1, index_rows == 0)
    shift_rows = jnp.where(is_fixed[None, :], 0, shift_rows)
    return (BLOCK * index_rows[None, :] + shift_rows).astype(jnp.int32)


def steps_of(own_key, extent, shards, smallest, top_value):
    def one(dim, parts):
        draws = jax.random.uniform(jax.random.fold_in(jax.random.fold_in(own_key, 6), dim), (parts,), jnp.float32, smallest / len(shards), top_value / len(shards))
        return jnp.repeat(jnp.exp(draws), extent[dim] // parts).reshape((-1,) + (1,) * (len(extent) - dim - 1))

    loudness = one(*shards[0])
    for cut in shards[1:]:
        loudness = loudness * one(*cut)
    return loudness


def bell_draw(rng, shape, width, limit, cuts=(), held_as=jnp.bfloat16):
    gain = steps_of(rng, shape, cuts, -0.22, 0.18) if cuts else 1.0
    result = jax.random.normal(rng, shape, jnp.float32) * width * gain
    return jnp.minimum(jnp.maximum(result, -limit), limit).astype(held_as)


def setup_inputs(seed: int = 0) -> dict:
    streams_of = jax.random.split(jax.random.key(seed), 5)
    vectors = bell_draw(streams_of[0], (NR, NC), 1.0, 6.0, ((0, 8), (1, 4)), jnp.float32)
    reflectors = draw_reflectors(jax.random.fold_in(streams_of[4], 71), 0)
    factors = draw_factors(jax.random.fold_in(streams_of[4], 71), 0)
    starts = draw_starts(jax.random.fold_in(streams_of[4], 71), 0)
    return dict(vectors=vectors, reflectors=reflectors, factors=factors, starts=starts)


highest = lax.Precision.HIGHEST

def apply_diamond(matrix, householder, factor, start_row):
    height = householder.shape[0]
    slab_rows = lax.dynamic_slice_in_dim(matrix, start_row, height, 0)
    projected = jnp.dot(householder.T.astype(jnp.float32), slab_rows.astype(jnp.float32), precision=highest, preferred_element_type=jnp.float32)
    scaled = jnp.dot(factor.astype(jnp.float32), projected.astype(jnp.float32), precision=highest, preferred_element_type=jnp.float32)
    slab_rows = slab_rows - jnp.dot(householder.astype(jnp.float32), scaled.astype(jnp.float32), precision=highest, preferred_element_type=jnp.float32)
    return lax.dynamic_update_slice_in_dim(matrix, slab_rows, start_row, 0)

def reference(vectors, reflectors, factors, starts):
    total_rows = vectors.shape[0]
    col_count = vectors.shape[1]
    diamond_count = starts.shape[1]
    padded = jnp.concatenate([vectors, jnp.zeros((BLOCK, col_count), jnp.float32)], 0)
    for tick_index in range(TICKS):
        tick_refl = reflectors[tick_index]
        tick_fact = factors[tick_index]
        tick_start = starts[tick_index]

        def apply_step(counter, matrix):
            which = diamond_count - 1 - counter
            householder = lax.dynamic_index_in_dim(tick_refl, which, 0, False)
            factor = lax.dynamic_index_in_dim(tick_fact, which, 0, False)
            start_row = lax.dynamic_index_in_dim(tick_start, which, 0, False)
            return apply_diamond(matrix, householder, factor, start_row)
        padded = lax.fori_loop(0, diamond_count, apply_step, padded)
        padded = jnp.concatenate([padded[:total_rows], jnp.zeros((BLOCK, col_count), jnp.float32)], 0)
    return padded[:total_rows]
```

```python
import functools

import jax
import jax.numpy as jnp
from jax import lax
from jax.experimental import pallas as pl
from jax.experimental.pallas import tpu as pltpu
from jax.sharding import PartitionSpec as P

MESH = pl.DeviceIdType.MESH
SHIFT = 64
CHUNKS = 4
f32, bf16 = jnp.float32, jnp.bfloat16


def split(x):
    high = x.astype(bf16)
    return high, (x - high.astype(f32)).astype(bf16)


def dot(a, b):
    return jnp.dot(a, b, preferred_element_type=f32)


def dot_nt(a, b):
    return lax.dot_general(a, b, (((1,), (1,)), ((), ())), preferred_element_type=f32)


def product(a, b):
    return times(a, *split(b))


def times(a, bh, bl):
    ah, al = split(a)
    return dot(ah, bh) + (dot(al, bh) + dot(ah, bl))


def kernel(
    n_rows, n_cols,
    vec_ref, pack_ref, start_ref, out_ref,
    gat, work, dense, shifted, inflow, head, outb, tailb, topb, lowb,
    vec_sem, own_sem, g_send, g_recv, p_send, p_recv, f_send, f_recv,
    i_send, j_send, i_recv, h_send, h_recv, t_send, t_recv,
):
    row = lax.axis_index("rows")
    col = lax.axis_index("cols")
    ticks, per, height, block = pack_ref.shape
    rows_here, width = vec_ref.shape
    n_dia = per * n_cols
    reach = height + SHIFT
    chunk = width // CHUNKS
    chips = n_cols // 2
    chip, core = lax.div(col, 2), lax.rem(col, 2)
    partner = chip * 2 + 1 - core
    above, below = lax.rem(row + n_rows - 1, n_rows), lax.rem(row + 1, n_rows)
    above2, below2 = lax.rem(row + n_rows - 2, n_rows), lax.rem(row + 2, n_rows)
    upper = lax.rem(row, 2) == 0
    last_pair = row >= n_rows - 2

    def peer_of(j):
        return lax.rem(chip + j, chips) * 2 + core

    def share(tick, owner):
        return gat.at[tick, pl.ds(owner * per, per)]

    vec_copy = pltpu.make_async_copy(
        vec_ref, work.at[0, pl.ds(0, rows_here)], vec_sem)
    vec_copy.start()

    def own_copy(tick):
        return pltpu.make_async_copy(pack_ref.at[tick], share(tick, col), own_sem.at[tick])

    barrier = pltpu.get_barrier_semaphore()
    for there in (above, below, above2, below2):
        pl.semaphore_signal(barrier, inc=1, device_id={"rows": there}, device_id_type=MESH)
    for j in range(1, chips):
        pl.semaphore_signal(barrier, inc=1, device_id={"cols": peer_of(j)}, device_id_type=MESH)
    pl.semaphore_signal(barrier, inc=1, device_id={"cols": partner}, device_id_type=MESH)
    pl.semaphore_wait(barrier, 4 + chips)

    def to_peer(tick, j, i):
        return pltpu.make_async_remote_copy(
            src_ref=pack_ref.at[tick, i], dst_ref=gat.at[tick, col * per + i],
            send_sem=g_send.at[tick, j - 1, i], recv_sem=g_recv.at[tick, j - 1, i],
            device_id={"cols": peer_of(j)}, device_id_type=MESH)

    def to_partner(tick):
        return pltpu.make_async_remote_copy(
            src_ref=pack_ref.at[tick], dst_ref=share(tick, col),
            send_sem=p_send.at[tick], recv_sem=p_recv.at[tick],
            device_id={"cols": partner}, device_id_type=MESH)

    def forward(tick, j, i):
        owner = lax.rem(chip + chips - j, chips) * 2 + core
        return pltpu.make_async_remote_copy(
            src_ref=gat.at[tick, owner * per + i], dst_ref=gat.at[tick, owner * per + i],
            send_sem=f_send.at[tick, j - 1, i], recv_sem=f_recv.at[tick, j - 1, i],
            device_id={"cols": partner}, device_id_type=MESH)

    @pl.loop(0, ticks)
    def _(tick):
        @pl.loop(0, per)
        def _(m):
            for j in range(1, chips):
                to_peer(tick, j, per - 1 - m).start()
        to_partner(tick).start()
        own_copy(tick).start()

    ii = lax.broadcasted_iota(jnp.int32, (block, block), 0)
    jj = lax.broadcasted_iota(jnp.int32, (block, block), 1)
    unit = jnp.where(ii == jj, 1.0, 0.0).astype(f32)
    zero = jnp.zeros((block, block), f32)
    total_rows = work.shape[1]

    def reset():
        spare = total_rows - rows_here
        work[:, pl.ds(rows_here, spare), :] = jnp.zeros((2, spare, block), f32)
        work[1, pl.ds(rows_here, block), :] = unit

    def clear_right():
        @pl.loop(0, rows_here // block)
        def _(i):
            work[1, pl.ds(pl.multiple_of(i * block, block), block), :] = zero

    clear_right()
    reset()
    shifted[...] = jnp.zeros_like(shifted)

    def in_block(tick, k):
        return jnp.clip(start_ref[tick, k] - row * rows_here - k * block, 0, SHIFT)

    def prepare(tick, k):
        slot = tick * n_dia + k
        top = gat[tick, k, pl.ds(0, block), :]
        lower = jnp.where(ii < jj, 0.0, jnp.where(ii > jj, top, unit))
        fh, fl = split(jnp.where(ii <= jj, top, 0.0))
        house = jnp.concatenate([lower, gat[tick, k, pl.ds(block, height - block), :]], 0)
        high, low = split(house)
        wide = dot(jnp.concatenate([high, low], 1), jnp.concatenate([fh, fh], 0))
        wh, wl = split(wide + dot(high, fl))
        full = dot_nt(jnp.concatenate([wh, wl], 1), jnp.concatenate([high, high], 1))
        dh, dl = split(full + dot_nt(wh, low))
        dense[slot, pl.ds(0, height)] = dh
        dense[slot, pl.ds(height, height)] = dl

    def prepare_share(tick, owner):
        @pl.loop(0, per, unroll=1)
        def _(i):
            prepare(tick, owner * per + i)

    def apply(tick, k):
        slot = tick * n_dia + k
        shift = in_block(tick, k)
        base = pl.multiple_of(k * block, block)
        slab = jnp.concatenate([work[h, pl.ds(base + shift, height), :] for h in (0, 1)], 1)
        sh, sl = split(slab)
        half = height // 2
        delta = jnp.concatenate([
            dot(dense[slot, pl.ds(p, half)], sh)
            + (dot(dense[slot, pl.ds(height + p, half)], sh) + dot(dense[slot, pl.ds(p, half)], sl))
            for p in (0, half)], 0)
        for h in (0, 1):
            shifted[h, pl.ds(SHIFT, height), :] = delta[:, h * block:(h + 1) * block]
        for h in (0, 1):
            work[h, pl.ds(base, reach), :] = (
                work[h, pl.ds(base, reach), :] - shifted[h, pl.ds(SHIFT - shift, reach), :])

    def send_up(tick, c, there, sems):
        part = pl.ds(c * chunk, chunk)
        return pltpu.make_async_remote_copy(
            src_ref=outb.at[tick, part], dst_ref=inflow.at[tick, part],
            send_sem=sems.at[tick, c], recv_sem=i_recv.at[tick, c],
            device_id={"rows": there}, device_id_type=MESH)

    def start_up(tick, c):
        send_up(tick, c, above2, i_send).start()
        send_up(tick, c, above, j_send).start()

    def pair_up(tick, m):
        return pltpu.make_async_remote_copy(
            src_ref=topb.at[tick, m], dst_ref=lowb.at[tick, m],
            send_sem=t_send.at[tick, m], recv_sem=t_recv.at[tick, m],
            device_id={"rows": above}, device_id_type=MESH)

    def send_down(tick):
        return pltpu.make_async_remote_copy(
            src_ref=tailb.at[tick], dst_ref=head.at[tick],
            send_sem=h_send.at[tick], recv_sem=h_recv.at[tick],
            device_id={"rows": below}, device_id_type=MESH)

    def take_head(tick):
        send_down(tick).wait_recv()
        work[0, pl.ds(0, block), :] = head[tick]

    @pl.loop(0, 2 * ticks)
    def _(m):
        mine = m < ticks
        tick = jnp.where(mine, m, m - ticks)

        @pl.when(mine)
        def _():
            own_copy(tick).wait()

        @pl.when(jnp.logical_not(mine))
        def _():
            to_partner(tick).wait_recv()

        prepare_share(tick, jnp.where(mine, col, partner))

    vec_copy.wait()

    @pl.loop(0, ticks)
    def _(tick):
        @pl.loop(0, n_dia)
        def _(counter):
            k = n_dia - 1 - counter
            owner, i = lax.div(k, per), lax.rem(k, per)
            o_chip, o_core = lax.div(owner, 2), lax.rem(owner, 2)
            j = lax.rem(chip + chips - o_chip, chips)

            @pl.when(j > 0)
            def _():
                @pl.when(o_core == 1)
                def _():
                    to_peer(tick, j, i).wait_recv()
                    forward(tick, j, i).start()

                @pl.when(o_core != core)
                def _():
                    forward(tick, j, i).wait_recv()

                prepare(tick, k)

            @pl.when(jnp.logical_and(k == 0, jnp.logical_and(row > 0, tick > 0)))
            def _():
                take_head(jnp.maximum(tick - 1, 0))

            apply(tick, k)

        edge = pl.ds(0, block)

        def correct(flow):
            tail = pl.ds(rows_here, block)
            fh, fl = split(flow)
            tailb[tick] = work[0, tail, :] + times(work[1, tail, :], fh, fl)
            send_down(tick).start()
            fcat = jnp.concatenate([fh, fh], 0)

            @pl.loop(0, rows_here // 256)
            def _(i):
                rows = pl.ds(pl.multiple_of(i * 256, 256), 256)
                rh, rl = split(work[1, rows, :])
                work[0, rows, :] = work[0, rows, :] + (
                    dot(jnp.concatenate([rh, rl], 1), fcat) + dot(rh, fl))

        @pl.when(jnp.logical_not(upper))
        def _():
            for m in (0, 1):
                topb[tick, m] = work[m, edge, :].T
            for m in (0, 1):
                pair_up(tick, m).start()

            @pl.when(jnp.logical_not(last_pair))
            def _():
                for c in range(CHUNKS):
                    send_up(tick, c, above, j_send).wait_recv()
                correct(inflow[tick].T)

        @pl.when(upper)
        def _():
            mh, ml = split(work[1, edge, :].T)
            outb[tick] = work[0, edge, :].T
            pair_up(tick, 0).wait_recv()
            outb[tick] = outb[tick] + times(lowb[tick, 0], mh, ml)

            @pl.when(last_pair)
            def _():
                @pl.when(row > 0)
                def _():
                    for c in range(CHUNKS):
                        start_up(tick, c)
                pair_up(tick, 1).wait_recv()
                correct(lowb[tick, 0].T)

            @pl.when(jnp.logical_not(last_pair))
            def _():
                pair_up(tick, 1).wait_recv()
                nh, nl = split(times(lowb[tick, 1], mh, ml))
                for c in range(CHUNKS):
                    send_up(tick, c, above2, i_send).wait_recv()

                    @pl.when(row > 0)
                    def _():
                        part = pl.ds(c * chunk, chunk)
                        outb[tick, part, :] = outb[tick, part, :] + times(
                            inflow[tick, part, :], nh, nl)
                        start_up(tick, c)

                lh, ll = split(lowb[tick, 1])
                correct((lowb[tick, 0] + times(inflow[tick], lh, ll)).T)

        @pl.when(tick < ticks - 1)
        def _():
            clear_right()
            reset()

    @pl.when(row > 0)
    def _():
        take_head(ticks - 1)

    out_copy = pltpu.make_async_copy(
        work.at[0, pl.ds(0, rows_here)], out_ref, vec_sem)
    out_copy.start()

    @pl.loop(0, ticks)
    def _(tick):
        @pl.loop(0, per)
        def _(i):
            for j in range(1, chips):
                to_peer(tick, j, i).wait_send()
                forward(tick, j, i).wait_send()
        to_partner(tick).wait_send()

        @pl.when(jnp.logical_and(upper, row > 0))
        def _():
            for c in range(CHUNKS):
                send_up(tick, c, above2, i_send).wait_send()
                send_up(tick, c, above, j_send).wait_send()

        @pl.when(jnp.logical_not(upper))
        def _():
            for m in (0, 1):
                pair_up(tick, m).wait_send()

        @pl.when(row < n_rows - 1)
        def _():
            send_down(tick).wait_send()

    out_copy.wait()


def solution(mesh):
    n_rows, n_cols = mesh.shape["rows"], mesh.shape["cols"]

    def on_device(vectors, reflectors, factors, starts):
        rows_here, width = vectors.shape
        ticks, per, height, block = reflectors.shape
        chips = n_cols // 2
        ii = lax.broadcasted_iota(jnp.int32, factors.shape, 2)
        jj = lax.broadcasted_iota(jnp.int32, factors.shape, 3)
        top = jnp.where(ii > jj, reflectors[:, :, :block], factors)
        packed = jnp.concatenate([top, reflectors[:, :, block:]], 2)
        dma = pltpu.SemaphoreType.DMA
        hops = max(chips - 1, 1)
        edge, flow = (ticks, block, width), (ticks, width, block)
        return pl.pallas_call(
            functools.partial(kernel, n_rows, n_cols),
            out_shape=jax.ShapeDtypeStruct(vectors.shape, f32),
            in_specs=[
                pl.BlockSpec(memory_space=pl.ANY),
                pl.BlockSpec(memory_space=pl.ANY),
                pl.BlockSpec(memory_space=pltpu.SMEM),
            ],
            out_specs=pl.BlockSpec(memory_space=pl.ANY),
            scratch_shapes=[
                pltpu.VMEM((ticks, per * n_cols, height, block), f32),
                pltpu.VMEM((2, rows_here + height - block + SHIFT, block), f32),
                pltpu.VMEM((ticks * per * n_cols, 2 * height, height), bf16),
                pltpu.VMEM((2, height + 2 * SHIFT, block), f32),
                pltpu.VMEM(flow, f32), pltpu.VMEM(edge, f32),
                pltpu.VMEM(flow, f32), pltpu.VMEM(edge, f32),
                pltpu.VMEM((ticks, 2, block, block), f32),
                pltpu.VMEM((ticks, 2, block, block), f32),
                dma, dma((ticks,)),
                dma((ticks, hops, per)), dma((ticks, hops, per)),
                dma((ticks,)), dma((ticks,)),
                dma((ticks, hops, per)), dma((ticks, hops, per)),
                dma((ticks, CHUNKS)), dma((ticks, CHUNKS)), dma((ticks, CHUNKS)),
                dma((ticks,)), dma((ticks,)), dma((ticks, 2)), dma((ticks, 2)),
            ],
            compiler_params=pltpu.CompilerParams(
                collective_id=0, has_side_effects=True, vmem_limit_bytes=36 * 2**20),
        )(vectors, packed, starts)

    return jax.shard_map(
        on_device,
        mesh=mesh,
        in_specs=(
            P("rows", "cols"),
            P(None, ("rows", "cols"), None, None),
            P(None, ("rows", "cols"), None, None),
            P(None, "rows"),
        ),
        out_specs=P("rows", "cols"),
        check_vma=False,
    )
```

```python
import functools

import jax
import jax.numpy as jnp
from jax import lax
from jax.experimental import pallas as pl
from jax.experimental.pallas import tpu as pltpu
from jax.sharding import PartitionSpec as P

MESH = pl.DeviceIdType.MESH
SHIFT = 64
CHUNKS = 2
f32, bf16 = jnp.float32, jnp.bfloat16


def split(x):
    high = x.astype(bf16)
    return high, (x - high.astype(f32)).astype(bf16)


def dot(a, b):
    return jnp.dot(a, b, preferred_element_type=f32)


def dot_nt(a, b):
    return lax.dot_general(a, b, (((1,), (1,)), ((), ())), preferred_element_type=f32)


def product(a, b):
    return times(a, *split(b))


def times(a, bh, bl):
    ah, al = split(a)
    return dot(ah, bh) + (dot(al, bh) + dot(ah, bl))


def kernel(
    n_rows, n_cols,
    vec_ref, refl_ref, fact_ref, start_ref, out_ref,
    gat, fact, work, dense, shifted, inflow, head, outb, tailb, topb, lowb, both,
    vec_sem, own_sem, fact_sem, g_send, g_recv, p_send, p_recv, f_send, f_recv,
    i_send, j_send, i_recv, h_send, h_recv, t_send, t_recv,
):
    row = lax.axis_index("rows")
    col = lax.axis_index("cols")
    ticks, per, height, block = refl_ref.shape
    rows_here, width = vec_ref.shape
    n_dia = per * n_cols
    reach = height + SHIFT
    chunk = width // CHUNKS
    chips = n_cols // 2
    chip, core = lax.div(col, 2), lax.rem(col, 2)
    partner = chip * 2 + 1 - core
    above, below = lax.rem(row + n_rows - 1, n_rows), lax.rem(row + 1, n_rows)
    above2, below2 = lax.rem(row + n_rows - 2, n_rows), lax.rem(row + 2, n_rows)
    upper = lax.rem(row, 2) == 0
    last_pair = row >= n_rows - 2

    def peer_of(j):
        return lax.rem(chip + j, chips) * 2 + core

    def share(tick, owner):
        return gat.at[tick, pl.ds(owner * per, per)]

    vec_copy = pltpu.make_async_copy(
        vec_ref, work.at[0, pl.ds(0, rows_here)], vec_sem)

    def own_copy(tick):
        return pltpu.make_async_copy(refl_ref.at[tick], share(tick, col), own_sem.at[tick])

    def fact_copy(tick):
        return pltpu.make_async_copy(fact_ref.at[tick], fact.at[tick], fact_sem.at[tick])

    @pl.loop(0, ticks)
    def _(tick):
        own_copy(tick).start()
        fact_copy(tick).start()

    vec_copy.start()

    barrier = pltpu.get_barrier_semaphore()
    for there in (above, below, above2, below2):
        pl.semaphore_signal(barrier, inc=1, device_id={"rows": there}, device_id_type=MESH)
    for j in range(1, chips):
        pl.semaphore_signal(barrier, inc=1, device_id={"cols": peer_of(j)}, device_id_type=MESH)
    pl.semaphore_signal(barrier, inc=1, device_id={"cols": partner}, device_id_type=MESH)
    pl.semaphore_wait(barrier, 4 + chips)

    def to_peer(tick, j, i):
        return pltpu.make_async_remote_copy(
            src_ref=gat.at[tick, col * per + i], dst_ref=gat.at[tick, col * per + i],
            send_sem=g_send.at[tick, j - 1, i], recv_sem=g_recv.at[tick, j - 1, i],
            device_id={"cols": peer_of(j)}, device_id_type=MESH)

    def to_partner(tick):
        return pltpu.make_async_remote_copy(
            src_ref=share(tick, col), dst_ref=share(tick, col),
            send_sem=p_send.at[tick], recv_sem=p_recv.at[tick],
            device_id={"cols": partner}, device_id_type=MESH)

    def forward(tick, j, i):
        owner = lax.rem(chip + chips - j, chips) * 2 + core
        return pltpu.make_async_remote_copy(
            src_ref=gat.at[tick, owner * per + i], dst_ref=gat.at[tick, owner * per + i],
            send_sem=f_send.at[tick, j - 1, i], recv_sem=f_recv.at[tick, j - 1, i],
            device_id={"cols": partner}, device_id_type=MESH)

    ii = lax.broadcasted_iota(jnp.int32, (block, block), 0)
    jj = lax.broadcasted_iota(jnp.int32, (block, block), 1)
    unit = jnp.where(ii == jj, 1.0, 0.0).astype(f32)
    zero = jnp.zeros((block, block), f32)

    @pl.loop(0, ticks)
    def _(tick):
        own_copy(tick).wait()
        fact_copy(tick).wait()

        @pl.loop(0, per)
        def _(m):
            k = col * per + per - 1 - m
            gat[tick, k, pl.ds(0, block), :] = jnp.where(
                ii > jj, gat[tick, k, pl.ds(0, block), :], fact[tick, per - 1 - m])

        @pl.loop(0, per)
        def _(m):
            for j in range(1, chips):
                to_peer(tick, j, per - 1 - m).start()
        to_partner(tick).start()

    total_rows = work.shape[1]

    def reset():
        spare = total_rows - rows_here
        work[:, pl.ds(rows_here, spare), :] = jnp.zeros((2, spare, block), f32)
        work[1, pl.ds(rows_here, block), :] = unit

    def clear_right():
        @pl.loop(0, rows_here // block)
        def _(i):
            work[1, pl.ds(pl.multiple_of(i * block, block), block), :] = zero

    clear_right()
    reset()
    shifted[...] = jnp.zeros_like(shifted)

    def in_block(tick, k):
        return jnp.clip(start_ref[tick, k] - row * rows_here - k * block, 0, SHIFT)

    def prepare(tick, k):
        slot = tick * n_dia + k
        top = gat[tick, k, pl.ds(0, block), :]
        lower = jnp.where(ii < jj, 0.0, jnp.where(ii > jj, top, unit))
        fh, fl = split(jnp.where(ii <= jj, top, 0.0))
        house = jnp.concatenate([lower, gat[tick, k, pl.ds(block, height - block), :]], 0)
        high, low = split(house)
        wide = dot(jnp.concatenate([high, low], 1), jnp.concatenate([fh, fh], 0))
        wh, wl = split(wide + dot(high, fl))
        full = dot_nt(jnp.concatenate([wh, wl], 1), jnp.concatenate([high, high], 1))
        dh, dl = split(full + dot_nt(wh, low))
        dense[slot, pl.ds(0, height)] = dh
        dense[slot, pl.ds(height, height)] = dl

    def prepare_share(tick, owner):
        @pl.loop(0, per, unroll=1)
        def _(i):
            prepare(tick, owner * per + i)

    def apply(tick, k):
        slot = tick * n_dia + k
        shift = in_block(tick, k)
        base = pl.multiple_of(k * block, block)
        slab = jnp.concatenate([work[h, pl.ds(base + shift, height), :] for h in (0, 1)], 1)
        sh, sl = split(slab)
        half = height // 2
        delta = jnp.concatenate([
            dot(dense[slot, pl.ds(p, half)], sh)
            + (dot(dense[slot, pl.ds(height + p, half)], sh) + dot(dense[slot, pl.ds(p, half)], sl))
            for p in (0, half)], 0)
        for h in (0, 1):
            shifted[h, pl.ds(SHIFT, height), :] = delta[:, h * block:(h + 1) * block]
        for h in (0, 1):
            work[h, pl.ds(base, reach), :] = (
                work[h, pl.ds(base, reach), :] - shifted[h, pl.ds(SHIFT - shift, reach), :])

    def send_up(tick, c, there, sems):
        part = pl.ds(c * chunk, chunk)
        return pltpu.make_async_remote_copy(
            src_ref=outb.at[tick, part], dst_ref=inflow.at[tick, part],
            send_sem=sems.at[tick, c], recv_sem=i_recv.at[tick, c],
            device_id={"rows": there}, device_id_type=MESH)

    def start_up(tick, c):
        send_up(tick, c, above2, i_send).start()
        send_up(tick, c, above, j_send).start()

    def pair_up(tick, m):
        return pltpu.make_async_remote_copy(
            src_ref=topb.at[tick, m], dst_ref=lowb.at[tick, m],
            send_sem=t_send.at[tick, m], recv_sem=t_recv.at[tick, m],
            device_id={"rows": above}, device_id_type=MESH)

    def send_down(tick):
        return pltpu.make_async_remote_copy(
            src_ref=tailb.at[tick], dst_ref=head.at[tick],
            send_sem=h_send.at[tick], recv_sem=h_recv.at[tick],
            device_id={"rows": below}, device_id_type=MESH)

    def take_head(tick):
        send_down(tick).wait_recv()
        work[0, pl.ds(0, block), :] = head[tick]

    def prepare_own(tick):
        @pl.loop(0, 2)
        def _(m):
            @pl.when(m == 1)
            def _():
                to_partner(tick).wait_recv()

            prepare_share(tick, jnp.where(m == 0, col, partner))

    prepare_own(0)
    vec_copy.wait()

    @pl.loop(0, ticks)
    def _(tick):
        @pl.loop(0, n_dia)
        def _(counter):
            k = n_dia - 1 - counter
            owner, i = lax.div(k, per), lax.rem(k, per)
            o_chip, o_core = lax.div(owner, 2), lax.rem(owner, 2)
            j = lax.rem(chip + chips - o_chip, chips)

            @pl.when(j > 0)
            def _():
                @pl.when(o_core == 1)
                def _():
                    to_peer(tick, j, i).wait_recv()
                    forward(tick, j, i).start()

                @pl.when(o_core != core)
                def _():
                    forward(tick, j, i).wait_recv()

                prepare(tick, k)

            @pl.when(jnp.logical_and(k == 0, jnp.logical_and(row > 0, tick > 0)))
            def _():
                take_head(jnp.maximum(tick - 1, 0))

            apply(tick, k)

        edge = pl.ds(0, block)

        def correct(flow):
            tail = pl.ds(rows_here, block)
            fh, fl = split(flow)
            tailb[tick] = work[0, tail, :] + times(work[1, tail, :], fh, fl)
            send_down(tick).start()
            fcat = jnp.concatenate([fh, fh], 0)

            span = 4 * block

            @pl.loop(0, rows_here // span)
            def _(i):
                rows = pl.ds(pl.multiple_of(i * span, span), span)
                rh, rl = split(work[1, rows, :])
                work[0, rows, :] = work[0, rows, :] + (
                    dot(jnp.concatenate([rh, rl], 1), fcat) + dot(rh, fl))
                work[1, rows, :] = jnp.zeros((span, block), f32)

        @pl.when(jnp.logical_not(upper))
        def _():
            for m in (0, 1):
                topb[tick, m] = work[m, edge, :].T
            for m in (0, 1):
                pair_up(tick, m).start()

        @pl.when(upper)
        def _():
            mh, ml = split(work[1, edge, :].T)
            outb[tick] = work[0, edge, :].T
            pair_up(tick, 0).wait_recv()
            outb[tick] = outb[tick] + times(lowb[tick, 0], mh, ml)

            @pl.when(jnp.logical_and(last_pair, row > 0))
            def _():
                for c in range(CHUNKS):
                    start_up(tick, c)

            pair_up(tick, 1).wait_recv()
            both[...] = times(lowb[tick, 1], mh, ml)

        @pl.when(tick < ticks - 1)
        def _():
            prepare_own(jnp.minimum(tick + 1, ticks - 1))

        @pl.when(jnp.logical_not(upper))
        def _():
            @pl.when(last_pair)
            def _():
                clear_right()

            @pl.when(jnp.logical_not(last_pair))
            def _():
                for c in range(CHUNKS):
                    send_up(tick, c, above, j_send).wait_recv()
                correct(inflow[tick].T)

        @pl.when(upper)
        def _():
            @pl.when(last_pair)
            def _():
                correct(lowb[tick, 0].T)

            @pl.when(jnp.logical_not(last_pair))
            def _():
                nh, nl = split(both[...])
                for c in range(CHUNKS):
                    send_up(tick, c, above2, i_send).wait_recv()

                    @pl.when(row > 0)
                    def _():
                        part = pl.ds(c * chunk, chunk)
                        outb[tick, part, :] = outb[tick, part, :] + times(
                            inflow[tick, part, :], nh, nl)
                        start_up(tick, c)

                lh, ll = split(lowb[tick, 1])
                correct((lowb[tick, 0] + times(inflow[tick], lh, ll)).T)

        @pl.when(tick < ticks - 1)
        def _():
            reset()

    @pl.when(row > 0)
    def _():
        take_head(ticks - 1)

    out_copy = pltpu.make_async_copy(
        work.at[0, pl.ds(0, rows_here)], out_ref, vec_sem)
    out_copy.start()

    @pl.loop(0, ticks)
    def _(tick):
        @pl.loop(0, per)
        def _(i):
            for j in range(1, chips):
                to_peer(tick, j, i).wait_send()
                forward(tick, j, i).wait_send()
        to_partner(tick).wait_send()

        @pl.when(jnp.logical_and(upper, row > 0))
        def _():
            for c in range(CHUNKS):
                send_up(tick, c, above2, i_send).wait_send()
                send_up(tick, c, above, j_send).wait_send()

        @pl.when(jnp.logical_not(upper))
        def _():
            for m in (0, 1):
                pair_up(tick, m).wait_send()

        @pl.when(row < n_rows - 1)
        def _():
            send_down(tick).wait_send()

    out_copy.wait()


def solution(mesh):
    n_rows, n_cols = mesh.shape["rows"], mesh.shape["cols"]

    def on_device(vectors, reflectors, factors, starts):
        rows_here, width = vectors.shape
        ticks, per, height, block = reflectors.shape
        chips = n_cols // 2
        dma = pltpu.SemaphoreType.DMA
        hops = max(chips - 1, 1)
        edge, flow = (ticks, block, width), (ticks, width, block)
        return pl.pallas_call(
            functools.partial(kernel, n_rows, n_cols),
            out_shape=jax.ShapeDtypeStruct(vectors.shape, f32),
            in_specs=[
                pl.BlockSpec(memory_space=pl.ANY),
                pl.BlockSpec(memory_space=pl.ANY),
                pl.BlockSpec(memory_space=pl.ANY),
                pl.BlockSpec(memory_space=pltpu.SMEM),
            ],
            out_specs=pl.BlockSpec(memory_space=pl.ANY),
            scratch_shapes=[
                pltpu.VMEM((ticks, per * n_cols, height, block), f32),
                pltpu.VMEM((ticks, per, block, block), f32),
                pltpu.VMEM((2, rows_here + height - block + SHIFT, block), f32),
                pltpu.VMEM((ticks * per * n_cols, 2 * height, height), bf16),
                pltpu.VMEM((2, height + 2 * SHIFT, block), f32),
                pltpu.VMEM(flow, f32), pltpu.VMEM(edge, f32),
                pltpu.VMEM(flow, f32), pltpu.VMEM(edge, f32),
                pltpu.VMEM((ticks, 2, block, block), f32),
                pltpu.VMEM((ticks, 2, block, block), f32),
                pltpu.VMEM((block, block), f32),
                dma, dma((ticks,)), dma((ticks,)),
                dma((ticks, hops, per)), dma((ticks, hops, per)),
                dma((ticks,)), dma((ticks,)),
                dma((ticks, hops, per)), dma((ticks, hops, per)),
                dma((ticks, CHUNKS)), dma((ticks, CHUNKS)), dma((ticks, CHUNKS)),
                dma((ticks,)), dma((ticks,)), dma((ticks, 2)), dma((ticks, 2)),
            ],
            compiler_params=pltpu.CompilerParams(
                collective_id=0, has_side_effects=True, vmem_limit_bytes=63 * 2**20),
        )(vectors, reflectors, factors, starts)

    return jax.shard_map(
        on_device,
        mesh=mesh,
        in_specs=(
            P("rows", "cols"),
            P(None, ("rows", "cols"), None, None),
            P(None, ("rows", "cols"), None, None),
            P(None, "rows"),
        ),
        out_specs=P("rows", "cols"),
        check_vma=False,
    )
```

```python
import functools

import jax
import jax.numpy as jnp
from jax import lax
from jax.experimental import pallas as pl
from jax.experimental.pallas import tpu as pltpu
from jax.sharding import PartitionSpec as P

MESH = pl.DeviceIdType.MESH
SHIFT = 64
CHUNKS = 2
f32, bf16 = jnp.float32, jnp.bfloat16


def split(x):
    high = x.astype(bf16)
    return high, (x - high.astype(f32)).astype(bf16)


def dot(a, b):
    return jnp.dot(a, b, preferred_element_type=f32)


def dot_nt(a, b):
    return lax.dot_general(a, b, (((1,), (1,)), ((), ())), preferred_element_type=f32)


def product(a, b):
    return times(a, *split(b))


def times(a, bh, bl):
    ah, al = split(a)
    return dot(ah, bh) + (dot(al, bh) + dot(ah, bl))


def kernel(
    n_rows, n_cols,
    vec_ref, refl_ref, fact_ref, start_ref, out_ref,
    gat, fact, work, dense, shifted, inflow, head, outb, tailb, topb, lowb, both,
    vec_sem, own_sem, fact_sem, g_send, g_recv, p_send, p_recv, f_send, f_recv,
    i_send, j_send, i_recv, h_send, h_recv, t_send, t_recv,
):
    row = lax.axis_index("rows")
    col = lax.axis_index("cols")
    ticks, per, height, block = refl_ref.shape
    rows_here, width = vec_ref.shape
    n_dia = per * n_cols
    reach = height + SHIFT
    chunk = width // CHUNKS
    chips = n_cols // 2
    chip, core = lax.div(col, 2), lax.rem(col, 2)
    partner = chip * 2 + 1 - core
    above, below = lax.rem(row + n_rows - 1, n_rows), lax.rem(row + 1, n_rows)
    above2, below2 = lax.rem(row + n_rows - 2, n_rows), lax.rem(row + 2, n_rows)
    upper = lax.rem(row, 2) == 0
    last_pair = row >= n_rows - 2

    def peer_of(j):
        return lax.rem(chip + j, chips) * 2 + core

    def share(tick, owner):
        return gat.at[tick, pl.ds(owner * per, per)]

    vec_copy = pltpu.make_async_copy(
        vec_ref, work.at[0, pl.ds(0, rows_here)], vec_sem)

    def own_copy(tick):
        return pltpu.make_async_copy(refl_ref.at[tick], share(tick, col), own_sem.at[tick])

    def fact_copy(tick):
        return pltpu.make_async_copy(fact_ref.at[tick], fact.at[tick], fact_sem.at[tick])

    @pl.loop(0, ticks)
    def _(tick):
        own_copy(tick).start()
        fact_copy(tick).start()

    vec_copy.start()

    barrier = pltpu.get_barrier_semaphore()
    for there in (above, below, above2, below2):
        pl.semaphore_signal(barrier, inc=1, device_id={"rows": there}, device_id_type=MESH)
    for j in range(1, chips):
        pl.semaphore_signal(barrier, inc=1, device_id={"cols": peer_of(j)}, device_id_type=MESH)
    pl.semaphore_signal(barrier, inc=1, device_id={"cols": partner}, device_id_type=MESH)
    pl.semaphore_wait(barrier, 4 + chips)

    def to_peer(tick, j, i):
        return pltpu.make_async_remote_copy(
            src_ref=gat.at[tick, col * per + i], dst_ref=gat.at[tick, col * per + i],
            send_sem=g_send.at[tick, j - 1, i], recv_sem=g_recv.at[tick, j - 1, i],
            device_id={"cols": peer_of(j)}, device_id_type=MESH)

    def to_partner(tick):
        return pltpu.make_async_remote_copy(
            src_ref=share(tick, col), dst_ref=share(tick, col),
            send_sem=p_send.at[tick], recv_sem=p_recv.at[tick],
            device_id={"cols": partner}, device_id_type=MESH)

    def forward(tick, j, i):
        owner = lax.rem(chip + chips - j, chips) * 2 + core
        return pltpu.make_async_remote_copy(
            src_ref=gat.at[tick, owner * per + i], dst_ref=gat.at[tick, owner * per + i],
            send_sem=f_send.at[tick, j - 1, i], recv_sem=f_recv.at[tick, j - 1, i],
            device_id={"cols": partner}, device_id_type=MESH)

    ii = lax.broadcasted_iota(jnp.int32, (block, block), 0)
    jj = lax.broadcasted_iota(jnp.int32, (block, block), 1)
    unit = jnp.where(ii == jj, 1.0, 0.0).astype(f32)
    zero = jnp.zeros((block, block), f32)

    @pl.loop(0, ticks)
    def _(tick):
        own_copy(tick).wait()
        fact_copy(tick).wait()

        @pl.loop(0, per)
        def _(m):
            k = col * per + per - 1 - m
            gat[tick, k, pl.ds(0, block), :] = jnp.where(
                ii > jj, gat[tick, k, pl.ds(0, block), :], fact[tick, per - 1 - m])

        @pl.loop(0, per)
        def _(m):
            for j in range(1, chips):
                to_peer(tick, j, per - 1 - m).start()
        to_partner(tick).start()

    total_rows = work.shape[1]

    def reset():
        spare = total_rows - rows_here
        work[:, pl.ds(rows_here, spare), :] = jnp.zeros((2, spare, block), f32)
        work[1, pl.ds(rows_here, block), :] = unit

    def clear_right():
        @pl.loop(0, rows_here // block)
        def _(i):
            work[1, pl.ds(pl.multiple_of(i * block, block), block), :] = zero

    clear_right()
    reset()
    shifted[...] = jnp.zeros_like(shifted)

    def in_block(tick, k):
        return jnp.clip(start_ref[tick, k] - row * rows_here - k * block, 0, SHIFT)

    def prepare(tick, k):
        slot = tick * n_dia + k
        top = gat[tick, k, pl.ds(0, block), :]
        lower = jnp.where(ii < jj, 0.0, jnp.where(ii > jj, top, unit))
        fh, fl = split(jnp.where(ii <= jj, top, 0.0))
        house = jnp.concatenate([lower, gat[tick, k, pl.ds(block, height - block), :]], 0)
        high, low = split(house)
        wide = dot(jnp.concatenate([high, low], 1), jnp.concatenate([fh, fh], 0))
        wh, wl = split(wide + dot(high, fl))
        full = dot_nt(jnp.concatenate([wh, wl], 1), jnp.concatenate([high, high], 1))
        dh, dl = split(full + dot_nt(wh, low))
        dense[slot, pl.ds(0, height)] = dh
        dense[slot, pl.ds(height, height)] = dl

    def prepare_share(tick, owner):
        @pl.loop(0, per, unroll=2 if per % 2 == 0 else 1)
        def _(i):
            prepare(tick, owner * per + i)

    def apply(tick, k):
        slot = tick * n_dia + k
        shift = in_block(tick, k)
        base = pl.multiple_of(k * block, block)
        slab = jnp.concatenate([work[h, pl.ds(base + shift, height), :] for h in (0, 1)], 1)
        sh, sl = split(slab)
        half = height // 2
        delta = jnp.concatenate([
            dot(dense[slot, pl.ds(p, half)], sh)
            + (dot(dense[slot, pl.ds(height + p, half)], sh) + dot(dense[slot, pl.ds(p, half)], sl))
            for p in (0, half)], 0)
        for h in (0, 1):
            shifted[h, pl.ds(SHIFT, height), :] = delta[:, h * block:(h + 1) * block]
        for h in (0, 1):
            work[h, pl.ds(base, reach), :] = (
                work[h, pl.ds(base, reach), :] - shifted[h, pl.ds(SHIFT - shift, reach), :])

    def send_up(tick, c, there, sems):
        part = pl.ds(c * chunk, chunk)
        return pltpu.make_async_remote_copy(
            src_ref=outb.at[tick, part], dst_ref=inflow.at[tick, part],
            send_sem=sems.at[tick, c], recv_sem=i_recv.at[tick, c],
            device_id={"rows": there}, device_id_type=MESH)

    def pair_up(tick, m):
        return pltpu.make_async_remote_copy(
            src_ref=topb.at[tick, m], dst_ref=lowb.at[tick, m],
            send_sem=t_send.at[tick, m], recv_sem=t_recv.at[tick, m],
            device_id={"rows": above}, device_id_type=MESH)

    def send_down(tick, m):
        return pltpu.make_async_remote_copy(
            src_ref=tailb.at[tick, m], dst_ref=head.at[tick, m],
            send_sem=h_send.at[tick, m], recv_sem=h_recv.at[tick, m],
            device_id={"rows": below}, device_id_type=MESH)

    def take_head(tick):
        for m in (0, 1):
            send_down(tick, m).wait_recv()
        edge = pl.ds(0, block)
        work[0, edge, :] = head[tick, 0] + product(head[tick, 1], work[0, edge, :])

    def prepare_own(tick):
        @pl.loop(0, 2)
        def _(m):
            @pl.when(m == 1)
            def _():
                to_partner(tick).wait_recv()

            prepare_share(tick, jnp.where(m == 0, col, partner))

    prepare_own(0)
    vec_copy.wait()

    @pl.loop(0, ticks)
    def _(tick):
        def turns(k):
            return lax.rem(chip + chips - lax.div(lax.div(k, per), 2), chips)

        def fetch(k):
            owner, i = lax.div(k, per), lax.rem(k, per)
            o_core = lax.rem(owner, 2)
            j = turns(k)

            @pl.when(o_core == 1)
            def _():
                to_peer(tick, j, i).wait_recv()
                forward(tick, j, i).start()

            @pl.when(o_core != core)
            def _():
                forward(tick, j, i).wait_recv()

        @pl.when(turns(n_dia - 1) > 0)
        def _():
            fetch(n_dia - 1)
            prepare(tick, n_dia - 1)

        @pl.loop(0, n_dia)
        def _(counter):
            k = n_dia - 1 - counter
            later = jnp.maximum(k - 1, 0)
            ahead = jnp.logical_and(k > 0, turns(later) > 0)

            @pl.when(ahead)
            def _():
                fetch(later)

            @pl.when(jnp.logical_and(k == 0, jnp.logical_and(row > 0, tick > 0)))
            def _():
                take_head(jnp.maximum(tick - 1, 0))

            @pl.when(ahead)
            def _():
                apply(tick, k)
                prepare(tick, later)

            @pl.when(jnp.logical_not(ahead))
            def _():
                apply(tick, k)

        edge = pl.ds(0, block)
        for m in (0, 1):
            tailb[tick, m] = work[m, pl.ds(rows_here, block), :]

        def correct(flow):
            fh, fl = split(flow)
            fcat = jnp.concatenate([fh, fh], 0)

            span = 4 * block

            @pl.loop(0, rows_here // span)
            def _(i):
                rows = pl.ds(pl.multiple_of(i * span, span), span)
                rh, rl = split(work[1, rows, :])
                work[0, rows, :] = work[0, rows, :] + (
                    dot(jnp.concatenate([rh, rl], 1), fcat) + dot(rh, fl))
                work[1, rows, :] = jnp.zeros((span, block), f32)

        @pl.when(jnp.logical_not(upper))
        def _():
            for m in (0, 1):
                topb[tick, m] = work[m, edge, :].T
            for m in (0, 1):
                pair_up(tick, m).start()

        @pl.when(upper)
        def _():
            mh, ml = split(work[1, edge, :].T)
            outb[tick] = work[0, edge, :].T
            pair_up(tick, 0).wait_recv()
            outb[tick] = outb[tick] + times(lowb[tick, 0], mh, ml)

            @pl.when(jnp.logical_and(last_pair, row > 0))
            def _():
                for c in range(CHUNKS):
                    send_up(tick, c, above2, i_send).start()
                for c in range(CHUNKS):
                    send_up(tick, c, above, j_send).start()

            pair_up(tick, 1).wait_recv()
            both[...] = times(lowb[tick, 1], mh, ml)

        @pl.when(row < n_rows - 1)
        def _():
            for m in (0, 1):
                send_down(tick, m).start()

        @pl.when(tick < ticks - 1)
        def _():
            prepare_own(jnp.minimum(tick + 1, ticks - 1))

        @pl.when(jnp.logical_not(upper))
        def _():
            @pl.when(last_pair)
            def _():
                clear_right()

            @pl.when(jnp.logical_not(last_pair))
            def _():
                for c in range(CHUNKS):
                    send_up(tick, c, above, j_send).wait_recv()
                correct(inflow[tick].T)

        @pl.when(upper)
        def _():
            @pl.when(last_pair)
            def _():
                correct(lowb[tick, 0].T)

            @pl.when(jnp.logical_not(last_pair))
            def _():
                nh, nl = split(both[...])
                for c in range(CHUNKS):
                    send_up(tick, c, above2, i_send).wait_recv()

                    @pl.when(row > 0)
                    def _():
                        part = pl.ds(c * chunk, chunk)
                        outb[tick, part, :] = outb[tick, part, :] + times(
                            inflow[tick, part, :], nh, nl)
                        send_up(tick, c, above2, i_send).start()

                @pl.when(row > 0)
                def _():
                    for c in range(CHUNKS):
                        send_up(tick, c, above, j_send).start()

                lh, ll = split(lowb[tick, 1])
                correct((lowb[tick, 0] + times(inflow[tick], lh, ll)).T)

        @pl.when(tick < ticks - 1)
        def _():
            reset()

    @pl.when(row > 0)
    def _():
        take_head(ticks - 1)

    out_copy = pltpu.make_async_copy(
        work.at[0, pl.ds(0, rows_here)], out_ref, vec_sem)
    out_copy.start()

    @pl.loop(0, ticks)
    def _(tick):
        @pl.loop(0, per)
        def _(i):
            for j in range(1, chips):
                to_peer(tick, j, i).wait_send()
                forward(tick, j, i).wait_send()
        to_partner(tick).wait_send()

        @pl.when(jnp.logical_and(upper, row > 0))
        def _():
            for c in range(CHUNKS):
                send_up(tick, c, above2, i_send).wait_send()
                send_up(tick, c, above, j_send).wait_send()

        @pl.when(jnp.logical_not(upper))
        def _():
            for m in (0, 1):
                pair_up(tick, m).wait_send()

        @pl.when(row < n_rows - 1)
        def _():
            for m in (0, 1):
                send_down(tick, m).wait_send()

    out_copy.wait()


def solution(mesh):
    n_rows, n_cols = mesh.shape["rows"], mesh.shape["cols"]

    def on_device(vectors, reflectors, factors, starts):
        rows_here, width = vectors.shape
        ticks, per, height, block = reflectors.shape
        chips = n_cols // 2
        dma = pltpu.SemaphoreType.DMA
        hops = max(chips - 1, 1)
        edge, flow = (ticks, 2, block, width), (ticks, width, block)
        return pl.pallas_call(
            functools.partial(kernel, n_rows, n_cols),
            out_shape=jax.ShapeDtypeStruct(vectors.shape, f32),
            in_specs=[pl.BlockSpec(memory_space=pltpu.HBM)] * 3
            + [pl.BlockSpec(memory_space=pltpu.SMEM)],
            out_specs=pl.BlockSpec(memory_space=pl.ANY),
            scratch_shapes=[
                pltpu.VMEM((ticks, per * n_cols, height, block), f32),
                pltpu.VMEM((ticks, per, block, block), f32),
                pltpu.VMEM((2, rows_here + height - block + SHIFT, block), f32),
                pltpu.VMEM((ticks * per * n_cols, 2 * height, height), bf16),
                pltpu.VMEM((2, height + 2 * SHIFT, block), f32),
                pltpu.VMEM(flow, f32), pltpu.VMEM(edge, f32),
                pltpu.VMEM(flow, f32), pltpu.VMEM(edge, f32),
                pltpu.VMEM((ticks, 2, block, block), f32),
                pltpu.VMEM((ticks, 2, block, block), f32),
                pltpu.VMEM((block, block), f32),
                dma, dma((ticks,)), dma((ticks,)),
                dma((ticks, hops, per)), dma((ticks, hops, per)),
                dma((ticks,)), dma((ticks,)),
                dma((ticks, hops, per)), dma((ticks, hops, per)),
                dma((ticks, CHUNKS)), dma((ticks, CHUNKS)), dma((ticks, CHUNKS)),
                dma((ticks, 2)), dma((ticks, 2)), dma((ticks, 2)), dma((ticks, 2)),
            ],
            compiler_params=pltpu.CompilerParams(
                collective_id=0, has_side_effects=True, vmem_limit_bytes=64900000),
        )(vectors, reflectors, factors, starts)

    return jax.shard_map(
        on_device,
        mesh=mesh,
        in_specs=(
            P("rows", "cols"),
            P(None, ("rows", "cols"), None, None),
            P(None, ("rows", "cols"), None, None),
            P(None, "rows"),
        ),
        out_specs=P("rows", "cols"),
        check_vma=False,
    )
```

```python
import functools

import jax
import jax.numpy as jnp
from jax import lax
from jax.experimental import pallas as pl
from jax.experimental.pallas import tpu as pltpu
from jax.sharding import PartitionSpec as P

MESH = pl.DeviceIdType.MESH
SHIFT = 64
CHUNKS = 4
f32, bf16 = jnp.float32, jnp.bfloat16


def split(x):
    high = x.astype(bf16)
    return high, (x - high.astype(f32)).astype(bf16)


def dot(a, b):
    return jnp.dot(a, b, preferred_element_type=f32)


def dot_nt(a, b):
    return lax.dot_general(a, b, (((1,), (1,)), ((), ())), preferred_element_type=f32)


def product(a, b):
    return times(a, *split(b))


def times(a, bh, bl):
    ah, al = split(a)
    return dot(ah, bh) + (dot(al, bh) + dot(ah, bl))


def kernel(
    n_rows, n_cols,
    vec_ref, refl_ref, fact_ref, start_ref, out_ref,
    gat, fact, work, dense, shifted, inflow, head, outb, tailb,
    vec_sem, own_sem, fact_sem, g_send, g_recv, p_send, p_recv, f_send, f_recv,
    i_send, i_recv, h_send, h_recv,
):
    row = lax.axis_index("rows")
    col = lax.axis_index("cols")
    ticks, per, height, block = refl_ref.shape
    rows_here, width = vec_ref.shape
    n_dia = per * n_cols
    reach = height + SHIFT
    chunk = width // CHUNKS
    chips = n_cols // 2
    chip, core = lax.div(col, 2), lax.rem(col, 2)
    partner = chip * 2 + 1 - core
    above, below = lax.rem(row + n_rows - 1, n_rows), lax.rem(row + 1, n_rows)

    def peer_of(j):
        return lax.rem(chip + j, chips) * 2 + core

    def share(tick, owner):
        return gat.at[tick, pl.ds(owner * per, per)]

    vec_copy = pltpu.make_async_copy(
        vec_ref, work.at[0, pl.ds(0, rows_here)], vec_sem)

    def own_copy(tick):
        return pltpu.make_async_copy(refl_ref.at[tick], share(tick, col), own_sem.at[tick])

    def fact_copy(tick):
        return pltpu.make_async_copy(fact_ref.at[tick], fact.at[tick], fact_sem.at[tick])

    @pl.loop(0, ticks)
    def _(tick):
        own_copy(tick).start()
        fact_copy(tick).start()

    vec_copy.start()

    barrier = pltpu.get_barrier_semaphore()
    for there in (above, below):
        pl.semaphore_signal(barrier, inc=1, device_id={"rows": there}, device_id_type=MESH)
    for j in range(1, chips):
        pl.semaphore_signal(barrier, inc=1, device_id={"cols": peer_of(j)}, device_id_type=MESH)
    pl.semaphore_signal(barrier, inc=1, device_id={"cols": partner}, device_id_type=MESH)
    pl.semaphore_wait(barrier, 2 + chips)

    def to_peer(tick, j, i):
        return pltpu.make_async_remote_copy(
            src_ref=gat.at[tick, col * per + i], dst_ref=gat.at[tick, col * per + i],
            send_sem=g_send.at[tick, j - 1, i], recv_sem=g_recv.at[tick, j - 1, i],
            device_id={"cols": peer_of(j)}, device_id_type=MESH)

    def to_partner(tick):
        return pltpu.make_async_remote_copy(
            src_ref=share(tick, col), dst_ref=share(tick, col),
            send_sem=p_send.at[tick], recv_sem=p_recv.at[tick],
            device_id={"cols": partner}, device_id_type=MESH)

    def forward(tick, j, i):
        owner = lax.rem(chip + chips - j, chips) * 2 + core
        return pltpu.make_async_remote_copy(
            src_ref=gat.at[tick, owner * per + i], dst_ref=gat.at[tick, owner * per + i],
            send_sem=f_send.at[tick, j - 1, i], recv_sem=f_recv.at[tick, j - 1, i],
            device_id={"cols": partner}, device_id_type=MESH)

    ii = lax.broadcasted_iota(jnp.int32, (block, block), 0)
    jj = lax.broadcasted_iota(jnp.int32, (block, block), 1)
    unit = jnp.where(ii == jj, 1.0, 0.0).astype(f32)
    zero = jnp.zeros((block, block), f32)

    @pl.loop(0, ticks)
    def _(tick):
        own_copy(tick).wait()
        fact_copy(tick).wait()

        @pl.loop(0, per)
        def _(m):
            k = col * per + per - 1 - m
            gat[tick, k, pl.ds(0, block), :] = jnp.where(
                ii > jj, gat[tick, k, pl.ds(0, block), :], fact[tick, per - 1 - m])

        @pl.loop(0, per)
        def _(m):
            for j in range(1, chips):
                to_peer(tick, j, per - 1 - m).start()
        to_partner(tick).start()

    total_rows = work.shape[1]

    def reset():
        spare = total_rows - rows_here
        work[:, pl.ds(rows_here, spare), :] = jnp.zeros((2, spare, block), f32)
        work[1, pl.ds(rows_here, block), :] = unit

    def clear_right():
        @pl.loop(0, rows_here // block)
        def _(i):
            work[1, pl.ds(pl.multiple_of(i * block, block), block), :] = zero

    clear_right()
    reset()
    shifted[...] = jnp.zeros_like(shifted)

    def in_block(tick, k):
        return jnp.clip(start_ref[tick, k] - row * rows_here - k * block, 0, SHIFT)

    def prepare(tick, k):
        slot = tick * n_dia + k
        top = gat[tick, k, pl.ds(0, block), :]
        lower = jnp.where(ii < jj, 0.0, jnp.where(ii > jj, top, unit))
        fh, fl = split(jnp.where(ii <= jj, top, 0.0))
        house = jnp.concatenate([lower, gat[tick, k, pl.ds(block, height - block), :]], 0)
        high, low = split(house)
        wide = dot(jnp.concatenate([high, low], 1), jnp.concatenate([fh, fh], 0))
        wh, wl = split(wide + dot(high, fl))
        full = dot_nt(jnp.concatenate([wh, wl], 1), jnp.concatenate([high, high], 1))
        dh, dl = split(full + dot_nt(wh, low))
        dense[slot, pl.ds(0, height)] = dh
        dense[slot, pl.ds(height, height)] = dl

    def prepare_share(tick, owner):
        @pl.loop(0, per, unroll=2 if per % 2 == 0 else 1)
        def _(i):
            prepare(tick, owner * per + i)

    def apply(tick, k):
        slot = tick * n_dia + k
        shift = in_block(tick, k)
        base = pl.multiple_of(k * block, block)
        slab = jnp.concatenate([work[h, pl.ds(base + shift, height), :] for h in (0, 1)], 1)
        sh, sl = split(slab)
        half = height // 2
        delta = jnp.concatenate([
            dot(dense[slot, pl.ds(p, half)], sh)
            + (dot(dense[slot, pl.ds(height + p, half)], sh) + dot(dense[slot, pl.ds(p, half)], sl))
            for p in (0, half)], 0)
        for h in (0, 1):
            shifted[h, pl.ds(SHIFT, height), :] = delta[:, h * block:(h + 1) * block]
        for h in (0, 1):
            work[h, pl.ds(base, reach), :] = (
                work[h, pl.ds(base, reach), :] - shifted[h, pl.ds(SHIFT - shift, reach), :])

    def send_up(tick, c):
        part = pl.ds(c * chunk, chunk)
        return pltpu.make_async_remote_copy(
            src_ref=outb.at[tick, part], dst_ref=inflow.at[tick, part],
            send_sem=i_send.at[tick, c], recv_sem=i_recv.at[tick, c],
            device_id={"rows": above}, device_id_type=MESH)

    def send_down(tick, m):
        return pltpu.make_async_remote_copy(
            src_ref=tailb.at[tick, m], dst_ref=head.at[tick, m],
            send_sem=h_send.at[tick, m], recv_sem=h_recv.at[tick, m],
            device_id={"rows": below}, device_id_type=MESH)

    def take_head(tick):
        for m in (0, 1):
            send_down(tick, m).wait_recv()
        edge = pl.ds(0, block)
        work[0, edge, :] = head[tick, 0] + product(head[tick, 1], work[0, edge, :])

    def prepare_own(tick):
        @pl.loop(0, 2)
        def _(m):
            @pl.when(m == 1)
            def _():
                to_partner(tick).wait_recv()

            prepare_share(tick, jnp.where(m == 0, col, partner))

    prepare_own(0)
    vec_copy.wait()

    @pl.loop(0, ticks)
    def _(tick):
        def turns(k):
            return lax.rem(chip + chips - lax.div(lax.div(k, per), 2), chips)

        def fetch(k):
            owner, i = lax.div(k, per), lax.rem(k, per)
            o_core = lax.rem(owner, 2)
            j = turns(k)

            @pl.when(o_core == 1)
            def _():
                to_peer(tick, j, i).wait_recv()
                forward(tick, j, i).start()

            @pl.when(o_core != core)
            def _():
                forward(tick, j, i).wait_recv()

        @pl.when(turns(n_dia - 1) > 0)
        def _():
            fetch(n_dia - 1)
            prepare(tick, n_dia - 1)

        @pl.loop(0, n_dia)
        def _(counter):
            k = n_dia - 1 - counter
            later = jnp.maximum(k - 1, 0)
            ahead = jnp.logical_and(k > 0, turns(later) > 0)

            @pl.when(ahead)
            def _():
                fetch(later)

            @pl.when(jnp.logical_and(k == 0, jnp.logical_and(row > 0, tick > 0)))
            def _():
                take_head(jnp.maximum(tick - 1, 0))

            @pl.when(ahead)
            def _():
                apply(tick, k)
                prepare(tick, later)

            @pl.when(jnp.logical_not(ahead))
            def _():
                apply(tick, k)

        edge = pl.ds(0, block)
        outb[tick] = work[0, edge, :].T

        @pl.when(row == n_rows - 1)
        def _():
            for c in range(CHUNKS):
                send_up(tick, c).start()
            clear_right()

        for m in (0, 1):
            tailb[tick, m] = work[m, pl.ds(rows_here, block), :]

        def correct(flow):
            fh, fl = split(flow)
            fcat = jnp.concatenate([fh, fh], 0)

            span = 4 * block

            @pl.loop(0, rows_here // span)
            def _(i):
                rows = pl.ds(pl.multiple_of(i * span, span), span)
                rh, rl = split(work[1, rows, :])
                work[0, rows, :] = work[0, rows, :] + (
                    dot(jnp.concatenate([rh, rl], 1), fcat) + dot(rh, fl))
                work[1, rows, :] = jnp.zeros((span, block), f32)

        @pl.when(row < n_rows - 1)
        def _():
            for m in (0, 1):
                send_down(tick, m).start()

        @pl.when(tick < ticks - 1)
        def _():
            prepare_own(jnp.minimum(tick + 1, ticks - 1))

        @pl.when(row < n_rows - 1)
        def _():
            mh, ml = split(work[1, edge, :].T)
            for c in range(CHUNKS):
                send_up(tick, c).wait_recv()

                @pl.when(row > 0)
                def _():
                    part = pl.ds(c * chunk, chunk)
                    outb[tick, part, :] = outb[tick, part, :] + times(
                        inflow[tick, part, :], mh, ml)
                    send_up(tick, c).start()

            correct(inflow[tick].T)

        @pl.when(tick < ticks - 1)
        def _():
            reset()

    @pl.when(row > 0)
    def _():
        take_head(ticks - 1)

    out_copy = pltpu.make_async_copy(
        work.at[0, pl.ds(0, rows_here)], out_ref, vec_sem)
    out_copy.start()

    @pl.loop(0, ticks)
    def _(tick):
        @pl.loop(0, per)
        def _(i):
            for j in range(1, chips):
                to_peer(tick, j, i).wait_send()
                forward(tick, j, i).wait_send()
        to_partner(tick).wait_send()

        @pl.when(row > 0)
        def _():
            for c in range(CHUNKS):
                send_up(tick, c).wait_send()

        @pl.when(row < n_rows - 1)
        def _():
            for m in (0, 1):
                send_down(tick, m).wait_send()

    out_copy.wait()


def solution(mesh):
    n_rows, n_cols = mesh.shape["rows"], mesh.shape["cols"]

    def on_device(vectors, reflectors, factors, starts):
        rows_here, width = vectors.shape
        ticks, per, height, block = reflectors.shape
        chips = n_cols // 2
        dma = pltpu.SemaphoreType.DMA
        hops = max(chips - 1, 1)
        edge, flow = (ticks, 2, block, width), (ticks, width, block)
        return pl.pallas_call(
            functools.partial(kernel, n_rows, n_cols),
            out_shape=jax.ShapeDtypeStruct(vectors.shape, f32),
            in_specs=[pl.BlockSpec(memory_space=pltpu.HBM)] * 3
            + [pl.BlockSpec(memory_space=pltpu.SMEM)],
            out_specs=pl.BlockSpec(memory_space=pl.ANY),
            scratch_shapes=[
                pltpu.VMEM((ticks, per * n_cols, height, block), f32),
                pltpu.VMEM((ticks, per, block, block), f32),
                pltpu.VMEM((2, rows_here + height - block + SHIFT, block), f32),
                pltpu.VMEM((ticks * per * n_cols, 2 * height, height), bf16),
                pltpu.VMEM((2, height + 2 * SHIFT, block), f32),
                pltpu.VMEM(flow, f32), pltpu.VMEM(edge, f32),
                pltpu.VMEM(flow, f32), pltpu.VMEM(edge, f32),
                dma, dma((ticks,)), dma((ticks,)),
                dma((ticks, hops, per)), dma((ticks, hops, per)),
                dma((ticks,)), dma((ticks,)),
                dma((ticks, hops, per)), dma((ticks, hops, per)),
                dma((ticks, CHUNKS)), dma((ticks, CHUNKS)),
                dma((ticks, 2)), dma((ticks, 2)),
            ],
            compiler_params=pltpu.CompilerParams(
                collective_id=0, has_side_effects=True, vmem_limit_bytes=40 * 2**20),
        )(vectors, reflectors, factors, starts)

    return jax.shard_map(
        on_device,
        mesh=mesh,
        in_specs=(
            P("rows", "cols"),
            P(None, ("rows", "cols"), None, None),
            P(None, ("rows", "cols"), None, None),
            P(None, "rows"),
        ),
        out_specs=P("rows", "cols"),
        check_vma=False,
    )
```

```python
import functools

import jax
import jax.numpy as jnp
from jax import lax
from jax.experimental import pallas as pl
from jax.experimental.pallas import tpu as pltpu
from jax.sharding import PartitionSpec as P

MESH = pl.DeviceIdType.MESH
SHIFT = 64
CHUNKS = 4
f32, bf16 = jnp.float32, jnp.bfloat16


def split(x):
    high = x.astype(bf16)
    return high, (x - high.astype(f32)).astype(bf16)


def dot(a, b):
    return jnp.dot(a, b, preferred_element_type=f32)


def dot_nt(a, b):
    return lax.dot_general(a, b, (((1,), (1,)), ((), ())), preferred_element_type=f32)


def product(a, b):
    return times(a, *split(b))


def times(a, bh, bl):
    ah, al = split(a)
    return dot(ah, bh) + (dot(al, bh) + dot(ah, bl))


def kernel(
    n_rows, n_cols,
    vec_ref, refl_ref, fact_ref, start_ref, out_ref,
    gat, fact, work, dense, shifted, inflow, head, outb, tailb,
    vec_sem, own_sem, fact_sem, g_send, g_recv, p_send, p_recv, f_send, f_recv,
    i_send, i_recv, h_send, h_recv,
):
    row = lax.axis_index("rows")
    col = lax.axis_index("cols")
    ticks, per, height, block = refl_ref.shape
    rows_here, width = vec_ref.shape
    n_dia = per * n_cols
    reach = height + SHIFT
    chunk = width // CHUNKS
    chips = n_cols // 2
    chip, core = lax.div(col, 2), lax.rem(col, 2)
    partner = chip * 2 + 1 - core
    above, below = lax.rem(row + n_rows - 1, n_rows), lax.rem(row + 1, n_rows)

    def peer_of(j):
        return lax.rem(chip + j, chips) * 2 + core

    def share(tick, owner):
        return gat.at[tick, pl.ds(owner * per, per)]

    vec_copy = pltpu.make_async_copy(
        vec_ref, work.at[0, pl.ds(0, rows_here)], vec_sem)

    def own_copy(tick):
        return pltpu.make_async_copy(refl_ref.at[tick], share(tick, col), own_sem.at[tick])

    def fact_copy(tick):
        return pltpu.make_async_copy(fact_ref.at[tick], fact.at[tick], fact_sem.at[tick])

    @pl.loop(0, ticks)
    def _(tick):
        own_copy(tick).start()
        fact_copy(tick).start()

    vec_copy.start()

    barrier = pltpu.get_barrier_semaphore()
    for there in (above, below):
        pl.semaphore_signal(barrier, inc=1, device_id={"rows": there}, device_id_type=MESH)
    for j in range(1, chips):
        pl.semaphore_signal(barrier, inc=1, device_id={"cols": peer_of(j)}, device_id_type=MESH)
    pl.semaphore_signal(barrier, inc=1, device_id={"cols": partner}, device_id_type=MESH)
    pl.semaphore_wait(barrier, 2 + chips)

    def to_peer(tick, j, i):
        return pltpu.make_async_remote_copy(
            src_ref=gat.at[tick, col * per + i], dst_ref=gat.at[tick, col * per + i],
            send_sem=g_send.at[tick, j - 1, i], recv_sem=g_recv.at[tick, j - 1, i],
            device_id={"cols": peer_of(j)}, device_id_type=MESH)

    def to_partner(tick):
        return pltpu.make_async_remote_copy(
            src_ref=share(tick, col), dst_ref=share(tick, col),
            send_sem=p_send.at[tick], recv_sem=p_recv.at[tick],
            device_id={"cols": partner}, device_id_type=MESH)

    def forward(tick, j, i):
        owner = lax.rem(chip + chips - j, chips) * 2 + core
        return pltpu.make_async_remote_copy(
            src_ref=gat.at[tick, owner * per + i], dst_ref=gat.at[tick, owner * per + i],
            send_sem=f_send.at[tick, j - 1, i], recv_sem=f_recv.at[tick, j - 1, i],
            device_id={"cols": partner}, device_id_type=MESH)

    ii = lax.broadcasted_iota(jnp.int32, (block, block), 0)
    jj = lax.broadcasted_iota(jnp.int32, (block, block), 1)
    unit = jnp.where(ii == jj, 1.0, 0.0).astype(f32)
    zero = jnp.zeros((block, block), f32)

    @pl.loop(0, ticks)
    def _(tick):
        own_copy(tick).wait()
        fact_copy(tick).wait()

        @pl.loop(0, per)
        def _(m):
            k = col * per + per - 1 - m
            gat[tick, k, pl.ds(0, block), :] = jnp.where(
                ii > jj, gat[tick, k, pl.ds(0, block), :], fact[tick, per - 1 - m])

        @pl.loop(0, per)
        def _(m):
            for j in range(1, chips):
                to_peer(tick, j, per - 1 - m).start()
        to_partner(tick).start()

    total_rows = work.shape[1]

    def reset():
        spare = total_rows - rows_here
        work[:, pl.ds(rows_here, spare), :] = jnp.zeros((2, spare, block), f32)
        work[1, pl.ds(rows_here, block), :] = unit

    def clear_right():
        @pl.loop(0, rows_here // block)
        def _(i):
            work[1, pl.ds(pl.multiple_of(i * block, block), block), :] = zero

    clear_right()
    reset()
    shifted[...] = jnp.zeros_like(shifted)

    def in_block(tick, k):
        return jnp.clip(start_ref[tick, k] - row * rows_here - k * block, 0, SHIFT)

    def prepare(tick, k):
        slot = tick * n_dia + k
        top = gat[tick, k, pl.ds(0, block), :]
        lower = jnp.where(ii < jj, 0.0, jnp.where(ii > jj, top, unit))
        fh, fl = split(jnp.where(ii <= jj, top, 0.0))
        house = jnp.concatenate([lower, gat[tick, k, pl.ds(block, height - block), :]], 0)
        high, low = split(house)
        wide = dot(jnp.concatenate([high, low], 1), jnp.concatenate([fh, fh], 0))
        wh, wl = split(wide + dot(high, fl))
        full = dot_nt(jnp.concatenate([wh, wl], 1), jnp.concatenate([high, high], 1))
        dh, dl = split(full + dot_nt(wh, low))
        dense[slot, pl.ds(0, height)] = dh
        dense[slot, pl.ds(height, height)] = dl

    def prepare_share(tick, owner):
        @pl.loop(0, per, unroll=2 if per % 2 == 0 else 1)
        def _(i):
            prepare(tick, owner * per + i)

    def apply(tick, k):
        slot = tick * n_dia + k
        shift = in_block(tick, k)
        base = pl.multiple_of(k * block, block)
        slab = jnp.concatenate([work[h, pl.ds(base + shift, height), :] for h in (0, 1)], 1)
        sh, sl = split(slab)
        half = height // 2
        delta = jnp.concatenate([
            dot(dense[slot, pl.ds(p, half)], sh)
            + (dot(dense[slot, pl.ds(height + p, half)], sh) + dot(dense[slot, pl.ds(p, half)], sl))
            for p in (0, half)], 0)
        for h in (0, 1):
            shifted[h, pl.ds(SHIFT, height), :] = delta[:, h * block:(h + 1) * block]
        for h in (0, 1):
            work[h, pl.ds(base, reach), :] = (
                work[h, pl.ds(base, reach), :] - shifted[h, pl.ds(SHIFT - shift, reach), :])

    def send_up(tick, c):
        part = pl.ds(c * chunk, chunk)
        return pltpu.make_async_remote_copy(
            src_ref=outb.at[tick, part], dst_ref=inflow.at[tick, part],
            send_sem=i_send.at[tick, c], recv_sem=i_recv.at[tick, c],
            device_id={"rows": above}, device_id_type=MESH)

    def send_down(tick, m):
        return pltpu.make_async_remote_copy(
            src_ref=tailb.at[tick, m], dst_ref=head.at[tick, m],
            send_sem=h_send.at[tick, m], recv_sem=h_recv.at[tick, m],
            device_id={"rows": below}, device_id_type=MESH)

    def take_head(tick):
        for m in (0, 1):
            send_down(tick, m).wait_recv()
        edge = pl.ds(0, block)
        work[0, edge, :] = head[tick, 0] + product(head[tick, 1], work[0, edge, :])

    def prepare_own(tick):
        @pl.loop(0, 2)
        def _(m):
            @pl.when(m == 1)
            def _():
                to_partner(tick).wait_recv()

            prepare_share(tick, jnp.where(m == 0, col, partner))

    @pl.loop(0, ticks)
    def _(tick):
        prepare_own(tick)

    vec_copy.wait()

    @pl.loop(0, ticks)
    def _(tick):
        def turns(k):
            return lax.rem(chip + chips - lax.div(lax.div(k, per), 2), chips)

        def fetch(k):
            owner, i = lax.div(k, per), lax.rem(k, per)
            o_core = lax.rem(owner, 2)
            j = turns(k)

            @pl.when(o_core == 1)
            def _():
                to_peer(tick, j, i).wait_recv()
                forward(tick, j, i).start()

            @pl.when(o_core != core)
            def _():
                forward(tick, j, i).wait_recv()

        @pl.when(turns(n_dia - 1) > 0)
        def _():
            fetch(n_dia - 1)
            prepare(tick, n_dia - 1)

        @pl.loop(0, n_dia)
        def _(counter):
            k = n_dia - 1 - counter
            later = jnp.maximum(k - 1, 0)
            ahead = jnp.logical_and(k > 0, turns(later) > 0)

            @pl.when(ahead)
            def _():
                fetch(later)

            @pl.when(jnp.logical_and(k == 0, jnp.logical_and(row > 0, tick > 0)))
            def _():
                take_head(jnp.maximum(tick - 1, 0))

            @pl.when(ahead)
            def _():
                apply(tick, k)
                prepare(tick, later)

            @pl.when(jnp.logical_not(ahead))
            def _():
                apply(tick, k)

        edge = pl.ds(0, block)
        outb[tick] = work[0, edge, :].T

        @pl.when(row == n_rows - 1)
        def _():
            for c in range(CHUNKS):
                send_up(tick, c).start()
            clear_right()

        for m in (0, 1):
            tailb[tick, m] = work[m, pl.ds(rows_here, block), :]

        def correct(flow):
            fh, fl = split(flow)
            fcat = jnp.concatenate([fh, fh], 0)

            span = 4 * block

            @pl.loop(0, rows_here // span)
            def _(i):
                rows = pl.ds(pl.multiple_of(i * span, span), span)
                rh, rl = split(work[1, rows, :])
                work[0, rows, :] = work[0, rows, :] + (
                    dot(jnp.concatenate([rh, rl], 1), fcat) + dot(rh, fl))
                work[1, rows, :] = jnp.zeros((span, block), f32)

        @pl.when(row < n_rows - 1)
        def _():
            for m in (0, 1):
                send_down(tick, m).start()

        @pl.when(row < n_rows - 1)
        def _():
            mh, ml = split(work[1, edge, :].T)
            for c in range(CHUNKS):
                send_up(tick, c).wait_recv()

                @pl.when(row > 0)
                def _():
                    part = pl.ds(c * chunk, chunk)
                    outb[tick, part, :] = outb[tick, part, :] + times(
                        inflow[tick, part, :], mh, ml)
                    send_up(tick, c).start()

            correct(inflow[tick].T)

        @pl.when(tick < ticks - 1)
        def _():
            reset()

    @pl.when(row > 0)
    def _():
        take_head(ticks - 1)

    out_copy = pltpu.make_async_copy(
        work.at[0, pl.ds(0, rows_here)], out_ref, vec_sem)
    out_copy.start()

    @pl.loop(0, ticks)
    def _(tick):
        @pl.loop(0, per)
        def _(i):
            for j in range(1, chips):
                to_peer(tick, j, i).wait_send()
                forward(tick, j, i).wait_send()
        to_partner(tick).wait_send()

        @pl.when(row > 0)
        def _():
            for c in range(CHUNKS):
                send_up(tick, c).wait_send()

        @pl.when(row < n_rows - 1)
        def _():
            for m in (0, 1):
                send_down(tick, m).wait_send()

    out_copy.wait()


def solution(mesh):
    n_rows, n_cols = mesh.shape["rows"], mesh.shape["cols"]

    def on_device(vectors, reflectors, factors, starts):
        rows_here, width = vectors.shape
        ticks, per, height, block = reflectors.shape
        chips = n_cols // 2
        dma = pltpu.SemaphoreType.DMA
        hops = max(chips - 1, 1)
        edge, flow = (ticks, 2, block, width), (ticks, width, block)
        return pl.pallas_call(
            functools.partial(kernel, n_rows, n_cols),
            out_shape=jax.ShapeDtypeStruct(vectors.shape, f32),
            in_specs=[pl.BlockSpec(memory_space=pltpu.HBM)] * 3
            + [pl.BlockSpec(memory_space=pltpu.SMEM)],
            out_specs=pl.BlockSpec(memory_space=pl.ANY),
            scratch_shapes=[
                pltpu.VMEM((ticks, per * n_cols, height, block), f32),
                pltpu.VMEM((ticks, per, block, block), f32),
                pltpu.VMEM((2, rows_here + height - block + SHIFT, block), f32),
                pltpu.VMEM((ticks * per * n_cols, 2 * height, height), bf16),
                pltpu.VMEM((2, height + 2 * SHIFT, block), f32),
                pltpu.VMEM(flow, f32), pltpu.VMEM(edge, f32),
                pltpu.VMEM(flow, f32), pltpu.VMEM(edge, f32),
                dma, dma((ticks,)), dma((ticks,)),
                dma((ticks, hops, per)), dma((ticks, hops, per)),
                dma((ticks,)), dma((ticks,)),
                dma((ticks, hops, per)), dma((ticks, hops, per)),
                dma((ticks, CHUNKS)), dma((ticks, CHUNKS)),
                dma((ticks, 2)), dma((ticks, 2)),
            ],
            compiler_params=pltpu.CompilerParams(
                collective_id=0, has_side_effects=True, vmem_limit_bytes=64900000),
        )(vectors, reflectors, factors, starts)

    return jax.shard_map(
        on_device,
        mesh=mesh,
        in_specs=(
            P("rows", "cols"),
            P(None, ("rows", "cols"), None, None),
            P(None, ("rows", "cols"), None, None),
            P(None, "rows"),
        ),
        out_specs=P("rows", "cols"),
        check_vma=False,
    )
```

```python
import functools

import jax
import jax.numpy as jnp
from jax import lax
from jax.experimental import pallas as pl
from jax.experimental.pallas import tpu as pltpu
from jax.sharding import PartitionSpec as P

MESH = pl.DeviceIdType.MESH
SHIFT = 64
CHUNKS = 4
f32, bf16 = jnp.float32, jnp.bfloat16


def split(x):
    high = x.astype(bf16)
    return high, (x - high.astype(f32)).astype(bf16)


def dot(a, b):
    return jnp.dot(a, b, preferred_element_type=f32)


def dot_nt(a, b):
    return lax.dot_general(a, b, (((1,), (1,)), ((), ())), preferred_element_type=f32)


def product(a, b):
    return times(a, *split(b))


def times(a, bh, bl):
    ah, al = split(a)
    return dot(ah, bh) + (dot(al, bh) + dot(ah, bl))


def kernel(
    n_rows, n_cols,
    vec_ref, refl_ref, fact_ref, start_ref, out_ref,
    gat, fact, flowh, flowl, work, dense, shifted, inflow, head, outb, tailb,
    vec_sem, own_sem, fact_sem, g_send, g_recv, p_send, p_recv, f_send, f_recv,
    i_send, i_recv, h_send, h_recv,
):
    row = lax.axis_index("rows")
    col = lax.axis_index("cols")
    ticks, per, height, block = refl_ref.shape
    rows_here, width = vec_ref.shape
    n_dia = per * n_cols
    reach = height + SHIFT
    chunk = width // CHUNKS
    chips = n_cols // 2
    chip, core = lax.div(col, 2), lax.rem(col, 2)
    partner = chip * 2 + 1 - core
    above, below = lax.rem(row + n_rows - 1, n_rows), lax.rem(row + 1, n_rows)

    def peer_of(j):
        return lax.rem(chip + j, chips) * 2 + core

    def share(tick, owner):
        return gat.at[tick, pl.ds(owner * per, per)]

    vec_copy = pltpu.make_async_copy(
        vec_ref, work.at[0, pl.ds(0, rows_here)], vec_sem)

    def own_copy(tick):
        return pltpu.make_async_copy(refl_ref.at[tick], share(tick, col), own_sem.at[tick])

    def fact_copy(tick):
        return pltpu.make_async_copy(fact_ref.at[tick], fact.at[tick], fact_sem.at[tick])

    @pl.loop(0, ticks)
    def _(tick):
        own_copy(tick).start()
        fact_copy(tick).start()

    vec_copy.start()

    barrier = pltpu.get_barrier_semaphore()
    for there in (above, below):
        pl.semaphore_signal(barrier, inc=1, device_id={"rows": there}, device_id_type=MESH)
    for j in range(1, chips):
        pl.semaphore_signal(barrier, inc=1, device_id={"cols": peer_of(j)}, device_id_type=MESH)
    pl.semaphore_signal(barrier, inc=1, device_id={"cols": partner}, device_id_type=MESH)
    pl.semaphore_wait(barrier, 2 + chips)

    def to_peer(tick, j, i):
        return pltpu.make_async_remote_copy(
            src_ref=gat.at[tick, col * per + i], dst_ref=gat.at[tick, col * per + i],
            send_sem=g_send.at[tick, j - 1, i], recv_sem=g_recv.at[tick, j - 1, i],
            device_id={"cols": peer_of(j)}, device_id_type=MESH)

    def to_partner(tick):
        return pltpu.make_async_remote_copy(
            src_ref=share(tick, col), dst_ref=share(tick, col),
            send_sem=p_send.at[tick], recv_sem=p_recv.at[tick],
            device_id={"cols": partner}, device_id_type=MESH)

    def forward(tick, j, i):
        owner = lax.rem(chip + chips - j, chips) * 2 + core
        return pltpu.make_async_remote_copy(
            src_ref=gat.at[tick, owner * per + i], dst_ref=gat.at[tick, owner * per + i],
            send_sem=f_send.at[tick, j - 1, i], recv_sem=f_recv.at[tick, j - 1, i],
            device_id={"cols": partner}, device_id_type=MESH)

    ii = lax.broadcasted_iota(jnp.int32, (block, block), 0)
    jj = lax.broadcasted_iota(jnp.int32, (block, block), 1)
    unit = jnp.where(ii == jj, 1.0, 0.0).astype(f32)
    zero = jnp.zeros((block, block), f32)

    @pl.loop(0, ticks)
    def _(tick):
        own_copy(tick).wait()
        fact_copy(tick).wait()

        @pl.loop(0, per)
        def _(m):
            k = col * per + per - 1 - m
            gat[tick, k, pl.ds(0, block), :] = jnp.where(
                ii > jj, gat[tick, k, pl.ds(0, block), :], fact[tick, per - 1 - m])

        @pl.loop(0, per)
        def _(m):
            for j in range(1, chips):
                to_peer(tick, j, per - 1 - m).start()
        to_partner(tick).start()

    total_rows = work.shape[1]

    def reset():
        spare = total_rows - rows_here
        work[:, pl.ds(rows_here, spare), :] = jnp.zeros((2, spare, block), f32)
        work[1, pl.ds(rows_here, block), :] = unit

    def clear_right():
        @pl.loop(0, rows_here // block)
        def _(i):
            work[1, pl.ds(pl.multiple_of(i * block, block), block), :] = zero

    clear_right()
    reset()
    shifted[...] = jnp.zeros_like(shifted)
    flowh[...] = jnp.zeros_like(flowh)
    flowl[...] = jnp.zeros_like(flowl)

    def in_block(tick, k):
        return jnp.clip(start_ref[tick, k] - row * rows_here - k * block, 0, SHIFT)

    def prepare(tick, k):
        slot = tick * n_dia + k
        top = gat[tick, k, pl.ds(0, block), :]
        lower = jnp.where(ii < jj, 0.0, jnp.where(ii > jj, top, unit))
        fh, fl = split(jnp.where(ii <= jj, top, 0.0))
        house = jnp.concatenate([lower, gat[tick, k, pl.ds(block, height - block), :]], 0)
        high, low = split(house)
        wide = dot(jnp.concatenate([high, low], 1), jnp.concatenate([fh, fh], 0))
        wh, wl = split(wide + dot(high, fl))
        full = dot_nt(jnp.concatenate([wh, wl], 1), jnp.concatenate([high, high], 1))
        dh, dl = split(full + dot_nt(wh, low))
        dense[slot, pl.ds(0, height)] = dh
        dense[slot, pl.ds(height, height)] = dl

    def prepare_share(tick, owner):
        @pl.loop(0, per, unroll=2 if per % 2 == 0 else 1)
        def _(i):
            prepare(tick, owner * per + i)

    def apply(tick, k):
        slot = tick * n_dia + k
        shift = in_block(tick, k)
        base = pl.multiple_of(k * block, block)
        slab = jnp.concatenate([work[h, pl.ds(base + shift, height), :] for h in (0, 1)], 1)
        sh, sl = split(slab)
        half = height // 2
        delta = jnp.concatenate([
            dot(dense[slot, pl.ds(p, half)], sh)
            + (dot(dense[slot, pl.ds(height + p, half)], sh) + dot(dense[slot, pl.ds(p, half)], sl))
            for p in (0, half)], 0)
        for h in (0, 1):
            shifted[h, pl.ds(SHIFT, height), :] = delta[:, h * block:(h + 1) * block]
        for h in (0, 1):
            work[h, pl.ds(base, reach), :] = (
                work[h, pl.ds(base, reach), :] - shifted[h, pl.ds(SHIFT - shift, reach), :])

    def send_up(tick, c):
        part = pl.ds(c * chunk, chunk)
        return pltpu.make_async_remote_copy(
            src_ref=outb.at[tick, part], dst_ref=inflow.at[tick, part],
            send_sem=i_send.at[tick, c], recv_sem=i_recv.at[tick, c],
            device_id={"rows": above}, device_id_type=MESH)

    def send_down(tick, m):
        return pltpu.make_async_remote_copy(
            src_ref=tailb.at[tick, m], dst_ref=head.at[tick, m],
            send_sem=h_send.at[tick, m], recv_sem=h_recv.at[tick, m],
            device_id={"rows": below}, device_id_type=MESH)

    def take_head(tick):
        for m in (0, 1):
            send_down(tick, m).wait_recv()
        edge = pl.ds(0, block)
        work[0, edge, :] = head[tick, 0] + product(head[tick, 1], work[0, edge, :])

    def prepare_own(tick):
        @pl.loop(0, 2)
        def _(m):
            @pl.when(m == 1)
            def _():
                to_partner(tick).wait_recv()

            prepare_share(tick, jnp.where(m == 0, col, partner))

    @pl.loop(0, ticks)
    def _(tick):
        prepare_own(tick)

    vec_copy.wait()

    @pl.loop(0, ticks)
    def _(tick):
        def turns(k):
            return lax.rem(chip + chips - lax.div(lax.div(k, per), 2), chips)

        def fetch(k):
            owner, i = lax.div(k, per), lax.rem(k, per)
            o_core = lax.rem(owner, 2)
            j = turns(k)

            @pl.when(o_core == 1)
            def _():
                to_peer(tick, j, i).wait_recv()
                forward(tick, j, i).start()

            @pl.when(o_core != core)
            def _():
                forward(tick, j, i).wait_recv()

        @pl.when(turns(n_dia - 1) > 0)
        def _():
            fetch(n_dia - 1)
            prepare(tick, n_dia - 1)

        def blend(k):
            rows = pl.ds(pl.multiple_of(k * block, block), block)
            rh, rl = split(work[1, rows, :])
            return rows, work[0, rows, :] + (
                dot(jnp.concatenate([rh, rl], 1), flowh[...]) + dot(rh, flowl[...]))

        def settle(rows, value):
            work[0, rows, :] = value
            work[1, rows, :] = zero

        settle(*blend(n_dia - 1))

        @pl.loop(0, n_dia)
        def _(counter):
            k = n_dia - 1 - counter
            later = jnp.maximum(k - 1, 0)
            remote = turns(later) > 0

            @pl.when(jnp.logical_and(k > 0, remote))
            def _():
                fetch(later)
                rows, value = blend(later)
                apply(tick, k)
                prepare(tick, later)
                settle(rows, value)

            @pl.when(jnp.logical_and(k > 0, jnp.logical_not(remote)))
            def _():
                rows, value = blend(later)
                apply(tick, k)
                settle(rows, value)

            @pl.when(k == 0)
            def _():
                @pl.when(jnp.logical_and(row > 0, tick > 0))
                def _():
                    take_head(jnp.maximum(tick - 1, 0))

                apply(tick, k)

        edge = pl.ds(0, block)
        outb[tick] = work[0, edge, :].T

        @pl.when(row == n_rows - 1)
        def _():
            for c in range(CHUNKS):
                send_up(tick, c).start()

        for m in (0, 1):
            tailb[tick, m] = work[m, pl.ds(rows_here, block), :]

        def correct():
            fcat, fl = flowh[...], flowl[...]
            span = 4 * block

            @pl.loop(0, rows_here // span)
            def _(i):
                rows = pl.ds(pl.multiple_of(i * span, span), span)
                rh, rl = split(work[1, rows, :])
                work[0, rows, :] = work[0, rows, :] + (
                    dot(jnp.concatenate([rh, rl], 1), fcat) + dot(rh, fl))

        @pl.when(row < n_rows - 1)
        def _():
            for m in (0, 1):
                send_down(tick, m).start()

        @pl.when(row < n_rows - 1)
        def _():
            mh, ml = split(work[1, edge, :].T)
            for c in range(CHUNKS):
                send_up(tick, c).wait_recv()

                @pl.when(row > 0)
                def _():
                    part = pl.ds(c * chunk, chunk)
                    outb[tick, part, :] = outb[tick, part, :] + times(
                        inflow[tick, part, :], mh, ml)
                    send_up(tick, c).start()

            fh, fl = split(inflow[tick].T)
            flowh[pl.ds(0, block), :] = fh
            flowh[pl.ds(block, block), :] = fh
            flowl[...] = fl

            @pl.when(tick == ticks - 1)
            def _():
                correct()

        @pl.when(tick < ticks - 1)
        def _():
            reset()

    @pl.when(row > 0)
    def _():
        take_head(ticks - 1)

    out_copy = pltpu.make_async_copy(
        work.at[0, pl.ds(0, rows_here)], out_ref, vec_sem)
    out_copy.start()

    @pl.loop(0, ticks)
    def _(tick):
        @pl.loop(0, per)
        def _(i):
            for j in range(1, chips):
                to_peer(tick, j, i).wait_send()
                forward(tick, j, i).wait_send()
        to_partner(tick).wait_send()

        @pl.when(row > 0)
        def _():
            for c in range(CHUNKS):
                send_up(tick, c).wait_send()

        @pl.when(row < n_rows - 1)
        def _():
            for m in (0, 1):
                send_down(tick, m).wait_send()

    out_copy.wait()


def solution(mesh):
    n_rows, n_cols = mesh.shape["rows"], mesh.shape["cols"]

    def on_device(vectors, reflectors, factors, starts):
        rows_here, width = vectors.shape
        ticks, per, height, block = reflectors.shape
        chips = n_cols // 2
        dma = pltpu.SemaphoreType.DMA
        hops = max(chips - 1, 1)
        edge, flow = (ticks, 2, block, width), (ticks, width, block)
        return pl.pallas_call(
            functools.partial(kernel, n_rows, n_cols),
            out_shape=jax.ShapeDtypeStruct(vectors.shape, f32),
            in_specs=[pl.BlockSpec(memory_space=pltpu.HBM)] * 3
            + [pl.BlockSpec(memory_space=pltpu.SMEM)],
            out_specs=pl.BlockSpec(memory_space=pl.ANY),
            scratch_shapes=[
                pltpu.VMEM((ticks, per * n_cols, height, block), f32),
                pltpu.VMEM((ticks, per, block, block), f32),
                pltpu.VMEM((2 * block, width), bf16), pltpu.VMEM((block, width), bf16),
                pltpu.VMEM((2, rows_here + height - block + SHIFT, block), f32),
                pltpu.VMEM((ticks * per * n_cols, 2 * height, height), bf16),
                pltpu.VMEM((2, height + 2 * SHIFT, block), f32),
                pltpu.VMEM(flow, f32), pltpu.VMEM(edge, f32),
                pltpu.VMEM(flow, f32), pltpu.VMEM(edge, f32),
                dma, dma((ticks,)), dma((ticks,)),
                dma((ticks, hops, per)), dma((ticks, hops, per)),
                dma((ticks,)), dma((ticks,)),
                dma((ticks, hops, per)), dma((ticks, hops, per)),
                dma((ticks, CHUNKS)), dma((ticks, CHUNKS)),
                dma((ticks, 2)), dma((ticks, 2)),
            ],
            compiler_params=pltpu.CompilerParams(
                collective_id=0, has_side_effects=True, vmem_limit_bytes=64900000),
        )(vectors, reflectors, factors, starts)

    return jax.shard_map(
        on_device,
        mesh=mesh,
        in_specs=(
            P("rows", "cols"),
            P(None, ("rows", "cols"), None, None),
            P(None, ("rows", "cols"), None, None),
            P(None, "rows"),
        ),
        out_specs=P("rows", "cols"),
        check_vma=False,
    )
```
